32 devices in a mesh: dp: 4 (over y, core), tensor: 8 (over z, x).
Axes of the slice: x: 2, y: 2, z: 4, core: 2. Of those that a mesh axis runs over, the one named last changes fastest.
Arguments:
- inputs: bfloat16 [12288, 5120], P('dp', 'tensor'), may hold values from -6 to 6
- cotangent: bfloat16 [12288, 4096], P('dp', 'tensor'), may hold values from -192 to 192
- lengths: int32 [32], P('dp'), may hold values from 96 to 384
- momentum: float32 [4, 4096, 5120], P('dp', 'tensor'), may hold values from -26 to 26
- weight: bfloat16 [4096, 5120], P('tensor'), may hold values from -0.00039863586 to 0.00039863586
- right_factor: float32 [5120, 64], replicated, may hold values from -1 to 1
Outputs:
- new_weight: bfloat16 [4096, 5120], P('tensor')
- new_momentum: float32 [4, 4096, 5120], P('dp', 'tensor')
- new_right: float32 [5120, 64], replicated
The draws below stay inside these ranges and needn't reach their ends.
Inputs may be any that keep to these rules, and one draw needn't show every extreme that they name: The first lengths[i] positions of block i are real tokens, the rest padding.
All inputs are finite; a program needn't handle non-finite values.
Results may differ from the reference program's by a relative error of at most 0.00045.
Values may be sent and summed in bfloat16 or wider, within the bound.
No kernel may reach another device: no remote copies, remote signals or barrier semaphores. Data moves between devices by JAX's collectives and lax.ppermute only.
A program may use at most 128 MiB of HBM per device.

```python
import math
import jax
import jax.numpy as jnp
from jax import lax

ROWS = 4096
COLS = 5120
RANK = 64
BLOCK = 384
BLOCKS = 8
REPLICAS = 4
TOKENS = 12288
ALL_BLOCKS = 32
N_DP = 4


def shared_factors(key):
    left_basis = jax.random.truncated_normal(jax.random.fold_in(key, 101), -4.0, 4.0, (ROWS, RANK), jnp.float32)
    right_basis = jax.random.truncated_normal(jax.random.fold_in(key, 102), -4.0, 4.0, (COLS, RANK), jnp.float32)
    return (left_basis, right_basis)


def draw_momentum(key, part):
    left_basis, right_basis = shared_factors(key)
    spread = math.log(3.0)
    jitter = jax.random.truncated_normal(jax.random.fold_in(key, 104), -6.0, 6.0, (REPLICAS, ROWS, COLS), jnp.float32)
    scales = jnp.exp(jax.random.uniform(jax.random.fold_in(key, 103), (RANK,), jnp.float32) * spread)
    amplitude = 2.5 / jnp.sqrt(jnp.sum(scales * scales))
    common = jnp.dot(left_basis * (scales * amplitude)[None, :], right_basis.T, precision=lax.Precision.HIGHEST)
    common = jnp.clip(common, -20.0, 20.0)
    return common[None] + jitter


def draw_right_factor(key, part):
    left_basis, right_basis = shared_factors(key)
    columns = right_basis / jnp.sqrt(jnp.sum(right_basis * right_basis, axis=0))[None, :]
    jitter = jax.random.truncated_normal(jax.random.fold_in(key, 201), -4.0, 4.0, (COLS, RANK), jnp.float32)
    return jnp.clip(columns + jitter * (0.5 / math.sqrt(COLS)), -1.0, 1.0)


def touch_ends(values, key, low, top_value):
    dims = values.shape
    spot = [jax.random.randint(jax.random.fold_in(key, axis), (), 0, dims[axis]) for axis in range(len(dims))]
    values = values.at[tuple(spot)].set(low)
    longest = dims.index(max(dims))
    spot[longest] = (spot[longest] + 1) % dims[longest]
    return values.at[tuple(spot)].set(top_value)


def steps_of(key, extent, cuts, least, largest):
    loudness, own = 1.0, jax.random.fold_in(key, 6)
    for dim, parts in cuts:
        heights = jnp.exp(jax.random.uniform(jax.random.fold_in(own, dim), (parts,), jnp.float32, least / len(cuts), largest / len(cuts)))
        loudness = loudness * jnp.repeat(heights, extent[dim] // parts).reshape([-1 if axis == dim else 1 for axis in range(len(extent))])
    return loudness


def centred(rng, extent, deviation, bound, cuts=(), held_as=jnp.bfloat16):
    values = deviation * jax.random.normal(rng, extent, jnp.float32)
    if cuts:
        values = values * steps_of(rng, extent, cuts, -0.22, 0.18)
    return jnp.clip(values, -bound, bound).astype(held_as)


def setup_inputs(seed: int = 0) -> dict:
    arg_keys = jax.random.split(jax.random.key(seed), 7)
    return {
        "inputs": centred(arg_keys[0], (TOKENS, COLS), 1.0, 6.0, ((0, 4), (1, 8))),
        "cotangent": centred(arg_keys[1], (TOKENS, ROWS), 32.0, 192.0, ((0, 4), (1, 8))),
        "lengths": touch_ends(jax.random.randint(arg_keys[2], (ALL_BLOCKS,), BLOCK // 4, BLOCK + 1), jax.random.fold_in(arg_keys[2], 1), BLOCK // 4, BLOCK).astype(jnp.int32),
        "momentum": draw_momentum(jax.random.fold_in(arg_keys[6], 71), 0),
        "weight": centred(arg_keys[4], (ROWS, COLS), 0.00006, 0.00039863586, ((0, 8),)),
        "right_factor": draw_right_factor(jax.random.fold_in(arg_keys[6], 71), 0),
    }


EPS = 1e-06
MU = 0.95
LR = 0.02

def reference(inputs, cotangent, lengths, momentum, weight, right_factor):
    hi = lax.Precision.HIGHEST
    per = BLOCKS * BLOCK
    position = jnp.arange(BLOCK, dtype=jnp.int32)
    keep = (position[None, :] < lengths[:, None]).reshape(-1).astype(jnp.bfloat16)
    masked = inputs * keep[:, None]
    counts = lax.optimization_barrier(jnp.sum(lengths.reshape(N_DP, BLOCKS).astype(jnp.float32), axis=1))
    boths = []
    total = jnp.zeros((ROWS, RANK), jnp.float32)
    for replica in range(N_DP):
        lower = replica * per
        grad = lax.dot_general(cotangent[lower:lower + per].astype(jnp.float32), masked[lower:lower + per].astype(jnp.float32), (((0,), (0,)), ((), ())), preferred_element_type=jnp.float32)
        both = momentum[replica] + grad / counts[replica]
        boths.append(both)
        total = total + jnp.dot(both, right_factor, precision=hi)
    left = total / N_DP
    gram = jnp.dot(left.T, left, precision=hi)
    factor = jnp.linalg.cholesky(gram)
    ortho = jax.scipy.linalg.solve_triangular(factor, left.T, lower=True).T
    right = jnp.zeros((COLS, RANK), jnp.float32)
    for replica in range(N_DP):
        right = right + lax.dot_general(boths[replica], ortho, (((0,), (0,)), ((), ())), precision=hi) / N_DP
    new_right = right * lax.rsqrt(lax.optimization_barrier(jnp.sum(right * right, axis=0)) + EPS)
    lowrank = jnp.dot(ortho, right.T, precision=hi)
    new_momentum = jnp.stack([both - (1.0 - MU) * lowrank for both in boths])
    update = jnp.dot(ortho, new_right.T, precision=hi)
    new_weight = (weight.astype(jnp.float32) - LR * math.sqrt(ROWS / COLS) * update).astype(jnp.bfloat16)
    return (new_weight, new_momentum, new_right)
```

```python
import functools
import math

import jax
import jax.numpy as jnp
from jax import lax
from jax.experimental import pallas as pl
from jax.experimental.pallas import tpu as pltpu
from jax.sharding import PartitionSpec as P

EPS = 1e-06
MU = 0.95
LR = 0.02
LANES = 128
PACK = 16
HI = lax.Precision.HIGHEST


def plain(inputs, cotangent, lengths, momentum, weight, right_factor):
    contract = (((0,), (0,)), ((), ()))
    replicas = lax.axis_size("dp")
    block_len = inputs.shape[0] // lengths.shape[0]
    position = jnp.arange(block_len, dtype=jnp.int32)
    keep = (position[None, :] < lengths[:, None]).reshape(-1).astype(jnp.bfloat16)
    masked = inputs * keep[:, None]
    count = jnp.sum(lengths.astype(jnp.float32))
    grad = lax.dot_general(
        cotangent,
        lax.all_gather(masked, "tensor", axis=1, tiled=True),
        contract,
        preferred_element_type=jnp.float32,
    )
    both = momentum[0] + grad / count
    left = lax.psum(jnp.dot(both, right_factor, precision=HI), "dp") / replicas
    gram = lax.psum(jnp.dot(left.T, left, precision=HI), "tensor")
    factor = jnp.linalg.cholesky(gram)
    ortho = jax.scipy.linalg.solve_triangular(factor, left.T, lower=True).T
    term = lax.dot_general(both, ortho, contract, precision=HI) / replicas
    right = lax.psum(term, ("dp", "tensor"))
    squares = jnp.sum(right * right, axis=0)
    new_right = right * lax.rsqrt(squares + EPS)
    lowrank = jnp.dot(ortho, right.T, precision=HI)
    new_momentum = (both - (1.0 - MU) * lowrank)[None]
    rows_all = ortho.shape[0] * lax.axis_size("tensor")
    update = jnp.dot(ortho, new_right.T, precision=HI)
    new_weight = (
        weight.astype(jnp.float32) - LR * math.sqrt(rows_all / right.shape[0]) * update
    ).astype(jnp.bfloat16)
    return (new_weight, new_momentum, new_right)


def pack_inputs_kernel(meta, x_ref, o_ref):
    blocks = meta.shape[0] // 2
    size = x_ref.shape[0] // blocks
    o_ref[...] = jnp.zeros_like(o_ref)
    row = lax.broadcasted_iota(jnp.int32, (size, x_ref.shape[1]), 0)
    for b in range(blocks):
        at = pl.multiple_of(meta[blocks + b], PACK)
        part = x_ref[b * size:(b + 1) * size, :]
        part = jnp.where(row < meta[b], part, jnp.zeros_like(part))
        o_ref[pl.ds(at, size), :] = part


def pack_inputs(x, meta):
    t, k = x.shape
    return pl.pallas_call(
        pack_inputs_kernel,
        out_shape=jax.ShapeDtypeStruct((t, k), x.dtype),
        grid_spec=pltpu.PrefetchScalarGridSpec(
            num_scalar_prefetch=1,
            grid=(k // LANES,),
            in_specs=[pl.BlockSpec((t, LANES), lambda i, m: (0, i))],
            out_specs=pl.BlockSpec((t, LANES), lambda i, m: (0, i)),
        ),
        cost_estimate=pl.CostEstimate(flops=t * k, bytes_accessed=4 * t * k, transcendentals=0),
        name="pack_inputs",
    )(meta, x)


def pack_cot_kernel(meta, c_ref, o_ref, buf):
    blocks = meta.shape[0] // 2
    t = c_ref.shape[0]
    size = t // blocks
    buf[...] = jnp.zeros_like(buf)
    for b in range(blocks):
        at = pl.multiple_of(meta[blocks + b], PACK)
        buf[pl.ds(at, size), :] = c_ref[b * size:(b + 1) * size, :]
    for i in range(t // LANES):
        o_ref[:, i * LANES:(i + 1) * LANES] = buf[i * LANES:(i + 1) * LANES, :].T


def pack_cot(c, meta):
    t, n = c.shape
    return pl.pallas_call(
        pack_cot_kernel,
        out_shape=jax.ShapeDtypeStruct((n, t), c.dtype),
        grid_spec=pltpu.PrefetchScalarGridSpec(
            num_scalar_prefetch=1,
            grid=(n // LANES,),
            in_specs=[pl.BlockSpec((t, LANES), lambda i, m: (0, i))],
            out_specs=pl.BlockSpec((LANES, t), lambda i, m: (i, 0)),
            scratch_shapes=[pltpu.VMEM((t, LANES), c.dtype)],
        ),
        cost_estimate=pl.CostEstimate(flops=t * n, bytes_accessed=4 * t * n, transcendentals=0),
        name="pack_cot",
    )(meta, c)


def finish_kernel(n, cols, a_ref, b_ref, mom_ref, *refs):
    own, got = refs[:n], refs[n:2 * n]
    out_ref = refs[-1]
    low = jnp.dot(a_ref[...], b_ref[...], preferred_element_type=jnp.float32)
    base = mom_ref[...] - (1.0 - MU) * low

    def put(parts):
        at = 0
        for part in parts:
            w = part.shape[1]
            out_ref[:, at:at + w] = base[:, at:at + w] + part[...]
            at += w

    @pl.when(pl.program_id(0) == 0)
    def _():
        put(own)

    @pl.when(pl.program_id(0) == 1)
    def _():
        put(got)


def finish(a, b, mom, own, got, cols, buf, tile):
    rows, depth = a.shape
    width = sum(v.shape[1] for v in own)
    n = len(own)
    parts = list(own) + list(got)
    specs = [
        pl.BlockSpec((tile, depth), lambda d, i, c: (i, 0)),
        pl.BlockSpec((depth, width), lambda d, i, c: (0, c[d])),
        pl.BlockSpec((tile, width), lambda d, i, c: (i, c[d])),
    ]
    specs += [pl.BlockSpec((tile, v.shape[1]), lambda d, i, c: (i, 0)) for v in parts]
    args = [a, b, mom] + parts
    aliases = {}
    if buf is not None:
        specs.append(pl.BlockSpec(memory_space=pl.ANY))
        aliases = {1 + len(args): 0}
        args.append(buf)
    return pl.pallas_call(
        functools.partial(finish_kernel, n),
        out_shape=jax.ShapeDtypeStruct(mom.shape, mom.dtype),
        grid_spec=pltpu.PrefetchScalarGridSpec(
            num_scalar_prefetch=1,
            grid=(2, rows // tile),
            in_specs=specs,
            out_specs=pl.BlockSpec((tile, width), lambda d, i, c: (i, c[d])),
        ),
        input_output_aliases=aliases,
        cost_estimate=pl.CostEstimate(
            flops=4 * rows * depth * width, bytes_accessed=24 * rows * width, transcendentals=0
        ),
        name="finish",
    )(cols, *args)


def update_kernel(step, a_ref, b_ref, w_ref, out_ref):
    low = jnp.dot(a_ref[...], b_ref[...], preferred_element_type=jnp.float32)
    out_ref[...] = (w_ref[...].astype(jnp.float32) - step * low).astype(out_ref.dtype)


def update(step, a, b, weight, width):
    rows, depth = a.shape
    cols = b.shape[1]
    return pl.pallas_call(
        functools.partial(update_kernel, step),
        out_shape=jax.ShapeDtypeStruct(weight.shape, weight.dtype),
        grid=(cols // width,),
        in_specs=[
            pl.BlockSpec((rows, depth), lambda i: (0, 0)),
            pl.BlockSpec((depth, width), lambda i: (0, i)),
            pl.BlockSpec((rows, width), lambda i: (0, i)),
        ],
        out_specs=pl.BlockSpec((rows, width), lambda i: (0, i)),
        cost_estimate=pl.CostEstimate(
            flops=2 * rows * depth * cols, bytes_accessed=4 * rows * cols, transcendentals=0
        ),
        name="update",
    )(a, b, weight)


def top(v):
    return lax.reduce_precision(v, 8, 7)


def split3(v):
    h = top(v)
    m = top(v - h)
    return jnp.concatenate([h, m, v - h - m], axis=0).astype(jnp.bfloat16)


def split2(v):
    h = top(v)
    return h.astype(jnp.bfloat16), (v - h).astype(jnp.bfloat16)


def dot3(v, w, dims=(((1,), (0,)), ((), ()))):
    n = v.shape[0]
    out = lax.dot_general(split3(v), w, dims, preferred_element_type=jnp.float32)
    return out[:n] + (out[n:2 * n] + out[2 * n:])


def pick(v, i):
    return lax.dynamic_index_in_dim(v, i, 0, keepdims=False)


def put_in_order(parts, me, n):
    stack = jnp.stack(parts[::-1] + parts[::-1][:-1])
    return lax.dynamic_slice_in_dim(stack, lax.rem(2 * n - 1 - me, n), n, 0)


class Grid:
    def __init__(self, size, reps):
        self.size, self.nz, self.reps = size, size // 2, reps
        self.me = lax.axis_index("tensor")
        self.z, self.x = self.me // 2, lax.rem(self.me, 2)
        self.r = lax.axis_index("dp")

    def swap(self, v, keep=None):
        pairs = [(t, t ^ 1) for t in range(self.size) if keep is None or keep(t // 2)]
        return lax.ppermute(v, "tensor", pairs)

    def zshift(self, v, k):
        n = self.nz
        pairs = [(2 * z + x, 2 * ((z + k) % n) + x) for z in range(n) for x in range(2)]
        return lax.ppermute(v, "tensor", pairs)

    def hop(self, v, step, sources):
        pairs = [(2 * z + x, 2 * (z + step) + x) for z in sources for x in range(2)]
        return lax.ppermute(v, "tensor", pairs)

    def rshift(self, v, k):
        n = self.reps
        return lax.ppermute(v, "dp", [(r, (r + k) % n) for r in range(n)])

    def z_scatter(self, v):
        n = self.nz
        acc = pick(v, self.z)
        for k in range(1, n):
            acc = acc + self.zshift(pick(v, lax.rem(self.z + k, n)), k)
        return acc

    def z_gather(self, v):
        parts = [v] + [self.zshift(v, k) for k in range(1, self.nz)]
        return put_in_order(parts, self.z, self.nz)

    def x_scatter(self, v):
        return pick(v, self.x) + self.swap(pick(v, 1 - self.x))

    def x_gather(self, v):
        other = self.swap(v)
        first = self.x == 0
        return jnp.stack([jnp.where(first, v, other), jnp.where(first, other, v)])

    def r_scatter(self, v):
        n = self.reps
        acc = pick(v, self.r)
        for k in range(1, n):
            acc = acc + self.rshift(pick(v, lax.rem(self.r + k, n)), k)
        return acc

    def r_gather(self, v):
        parts = [v] + [self.rshift(v, k) for k in range(1, self.reps)]
        return put_in_order(parts, self.r, self.reps)

    def r_sum(self, v):
        step = 1
        while step < self.reps:
            v = v + lax.ppermute(v, "dp", [(r, r ^ step) for r in range(self.reps)])
            step *= 2
        return v

    def r_max(self, v):
        return functools.reduce(jnp.maximum, [v] + [self.rshift(v, k) for k in range(1, self.reps)])

    def tensor_sum(self, v):
        n, t = v.shape
        part = self.x_scatter(v.reshape(2, n // 2, t))
        part = self.z_scatter(part.reshape(self.nz, n // self.size, t))
        part = self.z_gather(part).reshape(n // 2, t)
        return self.x_gather(part).reshape(n, t)

    def small_sum(self, v):
        v = v + self.swap(v)
        return jnp.sum(self.z_gather(v), axis=0)


def chunks_of(n):
    out, at = [], 0
    while at < n:
        w = min(2 * LANES, n - at)
        out.append((at, w))
        at += w
    return out


def body(t, packed, cot_t, lengths, momentum, weight, right_factor):
    reps, size = lax.axis_size("dp"), lax.axis_size("tensor")
    g = Grid(size, reps)
    nz = g.nz
    rows, cols = weight.shape
    rank = right_factor.shape[1]
    k = packed.shape[1]
    nq = k // LANES
    x_own = packed[:t]
    c_own = cot_t[:, :t]
    count = jnp.sum(lengths.astype(jnp.float32))
    scale = (1.0 / count)[None]
    mom = momentum[0]

    pieces = chunks_of(k)
    own = [x_own[:, at:at + w] for at, w in pieces]
    ups, downs = {0: own}, {0: own}
    for s in range(1, nz):
        ups[s] = [g.hop(v, 1, range(s - 1, nz - 1)) for v in ups[s - 1]]
        downs[s] = [g.hop(v, -1, range(1, nz - s + 1)) for v in downs[s - 1]]
    c_both = jnp.concatenate([c_own, g.swap(c_own)], axis=0)

    r_mine = lax.dynamic_slice_in_dim(right_factor, g.me * k, k, 0)
    last = (((1,), (1,)), ((), ()))
    xr = g.tensor_sum(dot3(r_mine.T, x_own, last))
    mom_r = lax.dot_general(right_factor, mom, (((0,), (1,)), ((), ())), precision=HI)
    left = g.r_sum(mom_r + dot3(xr, c_own, last) * scale) / reps
    gram = g.small_sum(lax.dot_general(left, left, last, precision=HI))
    factor = jnp.linalg.cholesky(gram)
    ortho = jax.scipy.linalg.solve_triangular(factor, left, lower=True)
    y = g.tensor_sum(dot3(ortho, c_own))
    term = jnp.dot(ortho, mom, precision=HI)
    nr = rank // reps
    term = g.r_scatter(term.reshape(reps, nr, cols))
    term = term.reshape(nr, size, k).transpose(1, 0, 2)
    term = term.reshape(nz, 2, nr, k).transpose(1, 0, 2, 3)
    term = g.z_scatter(g.x_scatter(term))
    xy = g.r_scatter((dot3(y, x_own) * scale).reshape(reps, nr, k))
    right = (term + xy) / reps
    right = g.x_gather(g.z_gather(right)).transpose(1, 0, 2, 3).reshape(size, nr, k)
    right = right.transpose(1, 0, 2).reshape(nr, cols)
    right = g.r_gather(right).reshape(rank, cols)
    new_right = right * lax.rsqrt(jnp.sum(right * right, axis=1) + EPS)[:, None]

    ah, am = split2(ortho)
    a = jnp.concatenate([ah, ah, am, am], axis=0).T
    rh, rm = split2(right)
    b = jnp.concatenate([rh, rm, rh, rm], axis=0)
    nh, nm = split2(new_right)
    bn = jnp.concatenate([nh, nm, nh, nm], axis=0)
    step = LR * math.sqrt(rows * size / cols)
    width = k
    new_weight = update(step, a, bn, weight, width)

    low_end, high_end = g.z == 0, g.z == nz - 1
    upper = g.z >= 2
    slots = [own]
    slots.append([jnp.where(low_end, d, u) for u, d in zip(ups[1], downs[1])])
    slots.append([jnp.where(upper, u, d) for u, d in zip(ups[2], downs[2])])
    slots.append(
        [
            jnp.where(low_end, d3, jnp.where(high_end, u3, d1))
            for u3, d3, d1 in zip(ups[3], downs[3], downs[1])
        ]
    )
    from_z = [
        g.z,
        jnp.where(low_end, 1, g.z - 1),
        jnp.where(upper, g.z - 2, g.z + 2),
        jnp.where(low_end, 3, jnp.where(high_end, 0, g.z + 1)),
    ]
    buf = None
    for parts, z in zip(slots, from_z):
        mine, got = [], []
        for v in parts:
            grad = jnp.dot(c_both, v, preferred_element_type=jnp.float32) * scale
            mine.append(grad[:rows])
            got.append(g.swap(grad[rows:]))
        at = jnp.stack([2 * z + g.x, 2 * z + 1 - g.x]).astype(jnp.int32)
        buf = finish(a, b, mom, mine, got, at, buf, rows // 2)
    return (new_weight, buf[None], new_right.T)


def sizes_of(t, low):
    unit = 2 * LANES
    out = [s for s in range(unit, t, unit) if s * 16 >= t * 10 and s >= low]
    return out + [t]


def per_device(inputs, cotangent, lengths, momentum, weight, right_factor):
    t, k = inputs.shape
    size, reps = lax.axis_size("tensor"), lax.axis_size("dp")
    rank = right_factor.shape[1]
    blocks = lengths.shape[0]
    fits = (
        size % 2 == 0
        and size == 8
        and reps & (reps - 1) == 0
        and k % LANES == 0
        and t % (2 * LANES) == 0
        and weight.shape[0] % (2 * LANES) == 0
        and rank % (8 * size) == 0
        and rank % (8 * reps) == 0
        and (t // blocks) % PACK == 0
    )
    args = (lengths, momentum, weight, right_factor)
    if not fits:
        return plain(inputs, cotangent, *args)
    held = (lengths + PACK - 1) // PACK * PACK
    ends = jnp.cumsum(held)
    g = Grid(size, reps)
    most = g.r_max(ends[-1:])[0]
    meta = jnp.concatenate([lengths, ends - held]).astype(jnp.int32)
    packed = pack_inputs(inputs, meta)
    cot_t = pack_cot(cotangent, meta)
    sizes = [t]
    which = sum((most > s).astype(jnp.int32) for s in sizes[:-1])
    if len(sizes) == 1:
        return body(t, packed, cot_t, *args)
    return lax.switch(
        which, [functools.partial(body, s) for s in sizes], packed, cot_t, *args
    )


def solution(mesh):
    placed = (
        P("dp", "tensor"),
        P("dp", "tensor"),
        P("dp"),
        P("dp", "tensor", None),
        P("tensor", None),
        P(),
    )
    return jax.shard_map(
        per_device,
        mesh=mesh,
        in_specs=placed,
        out_specs=(P("tensor", None), P("dp", "tensor", None), P()),
        check_vma=False,
    )
```
